32 devices in a mesh: ma: 2 (over y), fr: 4 (over x, core), fc: 4 (over z).
Axes of the slice: x: 2, y: 2, z: 4, core: 2. Of those that a mesh axis runs over, the one named last changes fastest.
Arguments:
- beam_transfer: bfloat16 [2, 256, 64, 512], P(None, ('ma', 'fr'), 'fc'), parts along dimension 1, may hold values from -0.25 to 0.25
- noise_var: float32 [256, 64], P(('ma', 'fr'), 'fc'), parts along dimension 0, may hold values from 0.3 to 30
- spectra: float32 [2, 512], replicated, may hold values from 0.05 to 5
- freq_covariance: float32 [2, 128, 128], replicated, as said below
- start_vectors: float32 [2, 256, 64, 128], P(None, ('ma', 'fr'), 'fc'), parts along dimension 1, may hold values from -6 to 6
Outputs:
- basis: float32 [2, 256, 64, 128], P(None, ('ma', 'fr'), 'fc'), parts along dimension 1
The draws below stay inside these ranges and needn't reach their ends.
There are 2 independent parts, one for each index of `ma`. The reference program is written for one: setup_inputs(seed, part) draws one part's arguments, and reference() takes and returns one part's arrays. A program takes and returns all parts, laid end to end along the dimension named above; an argument that names none is the same for every part. Nothing has to cross between parts.
Inputs may be any that keep to these rules, and one draw needn't show every extreme that they name: freq_covariance[k] is symmetric and positive definite for each k.
All inputs are finite; a program needn't handle non-finite values.
Results may differ from the reference program's by a relative error of at most 0.0071.
Values may be sent and summed in bfloat16 or wider, within the bound.
A program may use at most 192 MiB of HBM per device.

```python
import math
import jax
import jax.numpy as jnp
from jax import lax

F = 128
P_SIZE = 64
L = 512
R = 128
K = 2
ITERS = 2


def draw_freq_covariance(key, part):
    first, second = jax.random.split(jax.random.fold_in(key, 11))
    factor = jax.random.normal(first, (K, F, F), jnp.float32)
    diagonal = jax.random.uniform(second, (K, F), jnp.float32, 0.5, 1.5)
    symmetric = jnp.einsum('kab,kcb->kac', factor, factor) * (0.5 / F)
    return symmetric + diagonal[:, :, None] * jnp.eye(F, dtype=jnp.float32)[None]


def level_of(key, dims, cuts, low, top_value):
    factor_of, own = 1.0, jax.random.fold_in(key, 6)
    for dim, blocks in cuts:
        steps = jnp.exp(jax.random.uniform(jax.random.fold_in(own, dim), (blocks,), jnp.float32, low / len(cuts), top_value / len(cuts)))
        factor_of = factor_of * jnp.repeat(steps, dims[dim] // blocks).reshape([-1 if axis == dim else 1 for axis in range(len(dims))])
    return factor_of


def scatter_about(key, extent, scale, most, shards=(), held_as=jnp.bfloat16):
    loudness = level_of(key, extent, shards, -0.22, 0.18) if shards else 1.0
    values = jax.random.normal(key, extent, jnp.float32) * scale * loudness
    return jnp.minimum(jnp.maximum(values, -most), most).astype(held_as)


def setup_inputs(seed: int = 0, part: int = 0) -> dict:
    arg_keys = jax.random.split(jax.random.key(seed), 6)
    own_keys = jax.random.split(jax.random.fold_in(arg_keys[5], part), 6)
    return {
        "beam_transfer": scatter_about(own_keys[0], (2, F, P_SIZE, L), L ** -0.5, 0.25, ((1, 4), (2, 4))),
        "noise_var": jnp.clip(jnp.exp(math.log(30.0) - 4.6051701 * jax.random.uniform(own_keys[1], (F, P_SIZE), jnp.float32) ** level_of(own_keys[1], (F, P_SIZE), ((0, 4), (1, 4)), -0.2, 0.2)), 0.3, 30.0),
        "spectra": jnp.clip(jnp.exp(jax.random.uniform(arg_keys[2], (K, L), jnp.float32, math.log(0.05), math.log(5.0))), 0.05, 5.0),
        "freq_covariance": draw_freq_covariance(jax.random.fold_in(arg_keys[5], 71), part),
        "start_vectors": scatter_about(own_keys[4], (2, F, P_SIZE, R), 1.0, 6.0, ((1, 4), (2, 4)), jnp.float32),
    }


def row_operands(row_part, spectra):
    scaled = (row_part.astype(jnp.float32)[None] * spectra[:, None, None, :]).astype(jnp.bfloat16)
    real_rows = jnp.concatenate([scaled[:, 0], scaled[:, 1]], axis=-1)
    imag_rows = jnp.concatenate([scaled[:, 1], -scaled[:, 0]], axis=-1)
    return jnp.stack([real_rows, imag_rows], axis=1)

def apply_tile(pair_tile, vec_bf):
    row_count = pair_tile.shape[1]
    stacked = pair_tile.reshape(2 * row_count, pair_tile.shape[2])
    with_real = jnp.dot(stacked.astype(jnp.float32), vec_bf[0].astype(jnp.float32), preferred_element_type=jnp.float32)
    with_imag = jnp.dot(stacked.astype(jnp.float32), vec_bf[1].astype(jnp.float32), preferred_element_type=jnp.float32)
    real_part = with_real[:row_count] - with_imag[row_count:]
    imag_part = with_real[row_count:] + with_imag[:row_count]
    return jnp.stack([real_part, imag_part], axis=0)

def orthonormalize(image):
    gram_matrix = jnp.dot(image.T.astype(jnp.float32), image.astype(jnp.float32), precision=lax.Precision.HIGHEST, preferred_element_type=jnp.float32)
    lower = jnp.linalg.cholesky(gram_matrix)
    return lax.linalg.triangular_solve(lower, image, left_side=False, lower=True, transpose_a=True)

def reference(beam_transfer, noise_var, spectra, freq_covariance, start_vectors):
    whitened = (beam_transfer.astype(jnp.float32) * lax.rsqrt(noise_var)[None, :, :, None]).astype(jnp.bfloat16)
    order_all = F * P_SIZE
    col_operand = jnp.concatenate([whitened[0].reshape(order_all, L), whitened[1].reshape(order_all, L)], axis=-1)
    vectors = start_vectors
    for iteration in range(ITERS):
        vec_bf = vectors.astype(jnp.bfloat16).reshape(2, order_all, R)

        def block(freq):
            row_part = lax.dynamic_index_in_dim(whitened, freq, 1, keepdims=False)
            operand = row_operands(row_part, spectra)
            products = lax.dot_general(operand.astype(jnp.float32), col_operand.astype(jnp.float32), (((3,), (1,)), ((), ())), preferred_element_type=jnp.float32)
            cov_row = lax.dynamic_index_in_dim(freq_covariance, freq, 1, keepdims=False)
            weight = jnp.repeat(cov_row, P_SIZE, axis=1)
            pair_tile = jnp.einsum('kn,kcpn->cpn', weight, products).astype(jnp.bfloat16)
            return apply_tile(pair_tile, vec_bf)
        image = lax.map(block, jnp.arange(F, dtype=jnp.int32))
        image = jnp.transpose(image, (1, 0, 2, 3)).reshape(2 * order_all, R)
        vectors = orthonormalize(image).reshape(2, F, P_SIZE, R)
    return vectors * math.sqrt(2.0 * F * P_SIZE)
```

```python
import functools
import math

import jax
import jax.numpy as jnp
from jax import lax
from jax.experimental import pallas as pl
from jax.experimental.pallas import tpu as pltpu
from jax.sharding import PartitionSpec as P

ITERS = 2
MESH = pl.DeviceIdType.MESH
HIGHEST = lax.Precision.HIGHEST


def partner(me, step, count):
    if count & (count - 1):
        return lax.rem(step - me + count, count)
    total = 0
    bit = 1
    while bit < count:
        total = total + ((me // bit + step // bit) % 2) * bit
        bit *= 2
    return total


def kernel(
    nfr, nfc, own_modes, scale,
    w_ref, weight_ref, spec_ref, start_ref, out_ref,
    rows_ref, cols_ref, oper_ref, tile_ref, vec_ref, neg_ref, vsend_ref,
    rs_send, rs_recv, gram_send, gram_fr, gram_mid, gram_fc, elim_ref,
    rows_ss, rows_rs, cols_ss, cols_rs, vec_ss, vec_rs, rs_ss, rs_rs,
    gfr_ss, gfr_rs, gfc_ss, gfc_rs,
):
    me_r = lax.axis_index("fr")
    me_c = lax.axis_index("fc")
    own, depth = w_ref.shape[1], w_ref.shape[2]
    width = start_ref.shape[-1]
    block_rows = min(256, own)
    block_freqs = block_rows // own_modes

    def copy(src, dst, ss, rs, axis, peer):
        return pltpu.make_async_remote_copy(
            src_ref=src, dst_ref=dst, send_sem=ss, recv_sem=rs,
            device_id={axis: peer}, device_id_type=MESH,
        )

    barrier = pltpu.get_barrier_semaphore()
    for step in range(1, nfr):
        pl.semaphore_signal(barrier, inc=1, device_id={"fr": partner(me_r, step, nfr)}, device_id_type=MESH)
    for step in range(1, nfc):
        pl.semaphore_signal(barrier, inc=1, device_id={"fc": partner(me_c, step, nfc)}, device_id_type=MESH)
    pl.semaphore_wait(barrier, nfr + nfc - 2)

    def cols_copy(step, peer, slot):
        return copy(w_ref, cols_ref.at[slot], cols_ss.at[step - 1], cols_rs.at[step - 1], "fr", peer)

    def rows_copy(step, peer, slot):
        return copy(w_ref, rows_ref.at[slot], rows_ss.at[step - 1], rows_rs.at[step - 1], "fc", peer)

    def vec_copy(it, step, peer, slot):
        return copy(vsend_ref.at[it], vec_ref.at[it, slot], vec_ss.at[it, step - 1], vec_rs.at[it, step - 1], "fr", peer)

    for step in range(1, nfr):
        cols_copy(step, partner(me_r, step, nfr), me_r).start()
    for step in range(1, nfc):
        rows_copy(step, partner(me_c, step, nfc), me_c).start()
    vsend_ref[0, :, :width] = start_ref[0].astype(jnp.bfloat16)
    vsend_ref[0, :, width:] = start_ref[1].astype(jnp.bfloat16)
    for step in range(1, nfr):
        vec_copy(0, step, partner(me_r, step, nfr), me_r).start()
    rows_ref[me_c] = w_ref[...]
    cols_ref[me_r] = w_ref[...]

    def prepare(j):
        for k in range(2):
            spec = spec_ref[k : k + 1, :]
            real = (rows_ref[j, 0].astype(jnp.float32) * spec).astype(jnp.bfloat16)
            imag = (rows_ref[j, 1].astype(jnp.float32) * spec).astype(jnp.bfloat16)
            oper_ref[2 * k, :, :depth] = real
            oper_ref[2 * k, :, depth:] = imag
            oper_ref[2 * k + 1, :, :depth] = imag
            oper_ref[2 * k + 1, :, depth:] = -real

    def build(j, i):
        def part(b, carry):
            rows = pl.ds(pl.multiple_of(b * block_rows, block_rows), block_rows)
            left = oper_ref[:, rows, :].reshape(4 * block_rows, 2 * depth)
            prod = lax.dot_general(left[:, :depth], cols_ref[i, 0], (((1,), (1,)), ((), ())), preferred_element_type=jnp.float32)
            prod += lax.dot_general(left[:, depth:], cols_ref[i, 1], (((1,), (1,)), ((), ())), preferred_element_type=jnp.float32)
            prod = prod.reshape(4, block_rows, own)
            freqs = pl.ds(pl.multiple_of(b * block_freqs, block_freqs), block_freqs)
            first, second = (
                jnp.broadcast_to(weight_ref[i, k, freqs, :][:, None, :], (block_freqs, own_modes, own)).reshape(block_rows, own)
                for k in range(2)
            )
            for c in range(2):
                tile_ref[j, i, c, rows, :] = (first * prod[c] + second * prod[2 + c]).astype(jnp.bfloat16)
            return carry

        lax.fori_loop(0, own // block_rows, part, 0)

    prepare(me_c)
    build(me_c, me_r)

    def own_rows(step, carry):
        source = partner(me_r, step, nfr)
        cols_copy(step, source, source).wait_recv()
        build(me_c, source)
        return carry

    lax.fori_loop(1, nfr, own_rows, 0)

    def other_rows(step, carry):
        source = partner(me_c, step, nfc)
        rows_copy(step, source, source).wait_recv()
        prepare(source)

        def each(i, inner):
            build(source, i)
            return inner

        return lax.fori_loop(0, nfr, each, carry)

    lax.fori_loop(1, nfc, other_rows, 0)

    for it in range(ITERS):
        vec_ref[it, me_r] = vsend_ref[it]
        for step in range(1, nfr):
            source = partner(me_r, step, nfr)
            vec_copy(it, step, source, source).wait_recv()
        for i in range(nfr):
            neg_ref[i, :, :width] = -vec_ref[it, i, :, width:]
            neg_ref[i, :, width:] = vec_ref[it, i, :, :width]

        def apply(j):
            def term(i, total):
                total += jnp.dot(tile_ref[j, i, 0], vec_ref[it, i], preferred_element_type=jnp.float32)
                return total + jnp.dot(tile_ref[j, i, 1], neg_ref[i], preferred_element_type=jnp.float32)

            return lax.fori_loop(0, nfr, term, jnp.zeros((own, 2 * width), jnp.float32))

        def rs_copy(step, peer):
            return copy(rs_send.at[it, step - 1], rs_recv.at[it, step - 1], rs_ss.at[it, step - 1], rs_rs.at[it, step - 1], "fc", peer)

        def send_part(step, carry):
            peer = partner(me_c, step, nfc)
            rs_send[it, step - 1] = apply(peer).astype(jnp.bfloat16)
            rs_copy(step, peer).start()
            return carry

        lax.fori_loop(1, nfc, send_part, 0)
        image = apply(me_c)
        for step in range(1, nfc):
            rs_copy(step, partner(me_c, step, nfc)).wait_recv()
            image += rs_recv[it, step - 1].astype(jnp.float32)

        flat = jnp.concatenate([image[:, :width], image[:, width:]], axis=0)
        gram_send[it] = lax.dot_general(flat, flat, (((0,), (0,)), ((), ())), precision=HIGHEST, preferred_element_type=jnp.float32)

        def gfr_copy(step, peer, slot):
            return copy(gram_send.at[it], gram_fr.at[it, slot], gfr_ss.at[it, step - 1], gfr_rs.at[it, step - 1], "fr", peer)

        def gfc_copy(step, peer, slot):
            return copy(gram_mid.at[it], gram_fc.at[it, slot], gfc_ss.at[it, step - 1], gfc_rs.at[it, step - 1], "fc", peer)

        for step in range(1, nfr):
            gfr_copy(step, partner(me_r, step, nfr), me_r).start()
        gram_fr[it, me_r] = gram_send[it]
        for step in range(1, nfr):
            source = partner(me_r, step, nfr)
            gfr_copy(step, source, source).wait_recv()
        gram_mid[it] = jnp.sum(gram_fr[it], axis=0)
        for step in range(1, nfc):
            gfc_copy(step, partner(me_c, step, nfc), me_c).start()
        gram_fc[it, me_c] = gram_mid[it]
        for step in range(1, nfc):
            source = partner(me_c, step, nfc)
            gfc_copy(step, source, source).wait_recv()
        gram = jnp.sum(gram_fc[it], axis=0)

        row_id = lax.broadcasted_iota(jnp.int32, (width, 2 * width), 0)
        lane_id = lax.broadcasted_iota(jnp.int32, (width, 2 * width), 1)
        elim_ref[:, :width] = gram
        elim_ref[:, width:] = jnp.where(row_id[:, :width] == lane_id[:, :width], 1.0, 0.0)

        def eliminate(n, carry):
            row = elim_ref[pl.ds(n, 1), :]
            here = lane_id[:1, :width] == n
            pivot = jnp.sum(jnp.where(here, row[:, :width], 0.0), axis=1, keepdims=True)
            inv = 1.0 / jnp.sqrt(pivot)
            unit = row * inv
            column = jnp.sum(jnp.where(here, elim_ref[:, :width], 0.0), axis=1, keepdims=True)
            factor = jnp.where(row_id[:, :1] > n, column * inv, 0.0)
            elim_ref[...] = elim_ref[...] - factor * unit
            elim_ref[pl.ds(n, 1), :] = unit
            return carry

        lax.fori_loop(0, width, eliminate, 0)
        inverse = elim_ref[:, width:]
        vectors = lax.dot_general(flat, inverse, (((1,), (1,)), ((), ())), precision=HIGHEST, preferred_element_type=jnp.float32)
        if it + 1 < ITERS:
            vsend_ref[it + 1, :, :width] = vectors[:own].astype(jnp.bfloat16)
            vsend_ref[it + 1, :, width:] = vectors[own:].astype(jnp.bfloat16)
            for step in range(1, nfr):
                vec_copy(it + 1, step, partner(me_r, step, nfr), me_r).start()
        else:
            out_ref[0] = vectors[:own] * scale
            out_ref[1] = vectors[own:] * scale

    for step in range(1, nfr):
        peer = partner(me_r, step, nfr)
        cols_copy(step, peer, me_r).wait_send()
        for it in range(ITERS):
            vec_copy(it, step, peer, me_r).wait_send()
            gfr_copy_wait = copy(gram_send.at[it], gram_fr.at[it, me_r], gfr_ss.at[it, step - 1], gfr_rs.at[it, step - 1], "fr", peer)
            gfr_copy_wait.wait_send()
    for step in range(1, nfc):
        peer = partner(me_c, step, nfc)
        rows_copy(step, peer, me_c).wait_send()
        for it in range(ITERS):
            copy(rs_send.at[it, step - 1], rs_recv.at[it, step - 1], rs_ss.at[it, step - 1], rs_rs.at[it, step - 1], "fc", peer).wait_send()
            copy(gram_mid.at[it], gram_fc.at[it, me_c], gfc_ss.at[it, step - 1], gfc_rs.at[it, step - 1], "fc", peer).wait_send()


def body(nfr, nfc, beam_transfer, noise_var, spectra, freq_covariance, start_vectors):
    _, own_freqs, own_modes, depth = beam_transfer.shape
    own = own_freqs * own_modes
    width = start_vectors.shape[-1]
    order = own_freqs * nfr * own_modes * nfc
    whitened = (beam_transfer.astype(jnp.float32) * lax.rsqrt(noise_var)[None, :, :, None]).astype(jnp.bfloat16)
    row_cov = lax.dynamic_slice_in_dim(freq_covariance, lax.axis_index("fr") * own_freqs, own_freqs, 1)
    row_cov = row_cov.reshape(2, own_freqs, nfr, own_freqs)
    weight = jnp.transpose(jnp.repeat(row_cov, own_modes, axis=3), (2, 0, 1, 3))
    bf16, f32 = jnp.bfloat16, jnp.float32
    dma = pltpu.SemaphoreType.DMA
    scratch = [
        pltpu.VMEM((nfc, 2, own, depth), bf16),
        pltpu.VMEM((nfr, 2, own, depth), bf16),
        pltpu.VMEM((4, own, 2 * depth), bf16),
        pltpu.VMEM((nfc, nfr, 2, own, own), bf16),
        pltpu.VMEM((ITERS, nfr, own, 2 * width), bf16),
        pltpu.VMEM((nfr, own, 2 * width), bf16),
        pltpu.VMEM((ITERS, own, 2 * width), bf16),
        pltpu.VMEM((ITERS, nfc - 1, own, 2 * width), bf16),
        pltpu.VMEM((ITERS, nfc - 1, own, 2 * width), bf16),
        pltpu.VMEM((ITERS, width, width), f32),
        pltpu.VMEM((ITERS, nfr, width, width), f32),
        pltpu.VMEM((ITERS, width, width), f32),
        pltpu.VMEM((ITERS, nfc, width, width), f32),
        pltpu.VMEM((width, 2 * width), f32),
        dma((nfc - 1,)), dma((nfc - 1,)), dma((nfr - 1,)), dma((nfr - 1,)),
        dma((ITERS, nfr - 1)), dma((ITERS, nfr - 1)), dma((ITERS, nfc - 1)), dma((ITERS, nfc - 1)),
        dma((ITERS, nfr - 1)), dma((ITERS, nfr - 1)), dma((ITERS, nfc - 1)), dma((ITERS, nfc - 1)),
    ]
    vmem = pl.BlockSpec(memory_space=pltpu.VMEM)
    basis = pl.pallas_call(
        functools.partial(kernel, nfr, nfc, own_modes, math.sqrt(2.0 * order)),
        out_shape=jax.ShapeDtypeStruct((2, own, width), f32),
        in_specs=[vmem] * 4,
        out_specs=vmem,
        scratch_shapes=scratch,
        compiler_params=pltpu.CompilerParams(
            collective_id=0, has_side_effects=True, vmem_limit_bytes=60 * 1024 * 1024
        ),
    )(whitened.reshape(2, own, depth), weight, spectra, start_vectors.reshape(2, own, width))
    return basis.reshape(start_vectors.shape)


def solution(mesh):
    spec = P(None, ("ma", "fr"), "fc", None)
    in_specs = (spec, P(("ma", "fr"), "fc"), P(), P(), spec)
    run = functools.partial(body, mesh.shape["fr"], mesh.shape["fc"])
    return jax.shard_map(run, mesh=mesh, in_specs=in_specs, out_specs=spec, check_vma=False)
```

```python
import functools
import math

import jax
import jax.numpy as jnp
from jax import lax
from jax.experimental import pallas as pl
from jax.experimental.pallas import tpu as pltpu
from jax.sharding import PartitionSpec as P

ITERS = 2
MESH = pl.DeviceIdType.MESH
HIGHEST = lax.Precision.HIGHEST


PAIR = 2
PANEL = 32


def partner(me, step, count):
    total = 0
    bit = 1
    while bit < count:
        total = total + ((me // bit + step // bit) % 2) * bit
        bit *= 2
    return total


def kernel(
    nfr, nfc, own_modes, scale,
    w_ref, weight_ref, spec_ref, start_ref, out_ref,
    rows_ref, cols_ref, oper_ref, tile_ref, vec_ref, neg_ref, vsend_ref,
    rs_send, rs_recv, gram_send, gram_fr, gram_mid, gram_fc, elim_ref,
    rows_ss, rows_rs, cols_ss, cols_rs, vec_ss, vec_rs, rs_ss, rs_rs,
    gfr_ss, gfr_rs, gfc_ss, gfc_rs,
):
    me_r = lax.axis_index("fr")
    me_c = lax.axis_index("fc")
    own, depth = w_ref.shape[1], w_ref.shape[2]
    width = start_ref.shape[-1]
    block_rows = min(256, own)
    block_freqs = block_rows // own_modes
    ru, rv = PAIR, nfc // 2
    cu, cv = nfr // PAIR, 2
    row_count, col_count = ru * rv, cu * cv
    low_r, high_r = me_r % PAIR, me_r // PAIR
    low_c, high_c = me_c % rv, me_c // rv

    def row_peer(u, v):
        return {"fr": high_r * PAIR + partner(low_r, u, ru), "fc": high_c * rv + partner(low_c, v, rv)}

    def col_peer(u, v):
        return {"fr": partner(high_r, u, cu) * PAIR + low_r, "fc": partner(high_c, v, cv) * rv + low_c}

    def copy(src, dst, ss, rs, peer):
        return pltpu.make_async_remote_copy(
            src_ref=src, dst_ref=dst, send_sem=ss, recv_sem=rs, device_id=peer, device_id_type=MESH
        )

    barrier = pltpu.get_barrier_semaphore()
    greet = [{"fr": partner(me_r, step, nfr)} for step in range(1, nfr)]
    greet += [{"fc": partner(me_c, step, nfc)} for step in range(1, nfc)]
    greet += [row_peer(u, v) for u in range(1, ru) for v in range(1, rv)]
    for peer in greet:
        pl.semaphore_signal(barrier, inc=1, device_id=peer, device_id_type=MESH)
    pl.semaphore_wait(barrier, len(greet))

    def rows_copy(u, v, part):
        src = w_ref.at[part] if u == 0 or v == 0 else rows_ref.at[v * ru, part]
        slot = v * ru + u
        peer = row_peer(0, v) if u == 0 else row_peer(u, 0)
        return copy(src, rows_ref.at[slot, part], rows_ss.at[slot - 1, part], rows_rs.at[slot - 1, part], peer)

    def cols_copy(u, v, part):
        src = w_ref.at[part] if u == 0 or v == 0 else cols_ref.at[v * cu, part]
        slot = v * cu + u
        peer = col_peer(0, v) if u == 0 else col_peer(u, 0)
        return copy(src, cols_ref.at[slot, part], cols_ss.at[slot - 1, part], cols_rs.at[slot - 1, part], peer)

    def vec_copy(it, u, v):
        src = vsend_ref.at[it] if u == 0 or v == 0 else vec_ref.at[it, v * cu]
        slot = v * cu + u
        peer = col_peer(0, v) if u == 0 else col_peer(u, 0)
        return copy(src, vec_ref.at[it, slot], vec_ss.at[it, slot - 1], vec_rs.at[it, slot - 1], peer)

    def rs_copy(it, slot):
        return copy(
            rs_send.at[it, slot - 1], rs_recv.at[it, slot - 1], rs_ss.at[it, slot - 1], rs_rs.at[it, slot - 1],
            row_peer(slot % ru, slot // ru),
        )

    def gfr_copy(it, step):
        peer = partner(me_r, step, nfr)
        return copy(gram_send.at[it], gram_fr.at[it, me_r], gfr_ss.at[it, step - 1], gfr_rs.at[it, step - 1], {"fr": peer})

    def gfc_copy(it, step):
        peer = partner(me_c, step, nfc)
        return copy(gram_mid.at[it], gram_fc.at[it, me_c], gfc_ss.at[it, step - 1], gfc_rs.at[it, step - 1], {"fc": peer})

    def send_vectors(it):
        for v in range(1, cv):
            vec_copy(it, 0, v).start()
        for u in range(1, cu):
            vec_copy(it, u, 0).start()
        vec_ref[it, 0] = vsend_ref[it]

    def pass_vectors(it):
        for v in range(1, cv):
            vec_copy(it, 0, v).wait_recv()
            for u in range(1, cu):
                vec_copy(it, u, v).start()

    for v in range(1, cv):
        for part in range(2):
            cols_copy(0, v, part).start()
    for u in range(1, cu):
        for part in range(2):
            cols_copy(u, 0, part).start()
    for u in range(1, ru):
        for part in range(2):
            rows_copy(u, 0, part).start()
    for v in range(1, rv):
        for part in range(2):
            rows_copy(0, v, part).start()
    vsend_ref[0, :, :width] = start_ref[0].astype(jnp.bfloat16)
    vsend_ref[0, :, width:] = start_ref[1].astype(jnp.bfloat16)
    send_vectors(0)
    rows_ref[0] = w_ref[...]
    cols_ref[0] = w_ref[...]

    def prepare(j):
        for k in range(2):
            spec = spec_ref[k : k + 1, :]
            real = (rows_ref[j, 0].astype(jnp.float32) * spec).astype(jnp.bfloat16)
            imag = (rows_ref[j, 1].astype(jnp.float32) * spec).astype(jnp.bfloat16)
            oper_ref[j, 2 * k, :, :depth] = real
            oper_ref[j, 2 * k, :, depth:] = imag
            oper_ref[j, 2 * k + 1, :, :depth] = imag
            oper_ref[j, 2 * k + 1, :, depth:] = -real

    def build(j, i):
        row_weight = partner(low_r, j % ru, ru)
        col_weight = partner(high_r, i % cu, cu)

        def part(b, carry):
            rows = pl.ds(pl.multiple_of(b * block_rows, block_rows), block_rows)
            left = oper_ref[j, :, rows, :].reshape(4 * block_rows, 2 * depth)
            prod = lax.dot_general(left[:, :depth], cols_ref[i, 0], (((1,), (1,)), ((), ())), preferred_element_type=jnp.float32)
            prod += lax.dot_general(left[:, depth:], cols_ref[i, 1], (((1,), (1,)), ((), ())), preferred_element_type=jnp.float32)
            prod = prod.reshape(4, block_rows, own)
            freqs = pl.ds(pl.multiple_of(b * block_freqs, block_freqs), block_freqs)
            first, second = (
                jnp.broadcast_to(
                    weight_ref[row_weight, col_weight, k, freqs, :][:, None, :], (block_freqs, own_modes, own)
                ).reshape(block_rows, own)
                for k in range(2)
            )
            for c in range(2):
                tile_ref[j, i, c, rows, :] = (first * prod[c] + second * prod[2 + c]).astype(jnp.bfloat16)
            return carry

        lax.fori_loop(0, own // block_rows, part, 0)

    def build_all(row_low, row_high, col_low, col_high):
        def per_col(i, carry):
            def per_row(j, inner):
                build(j, i)
                return inner

            return lax.fori_loop(row_low, row_high, per_row, carry)

        lax.fori_loop(col_low, col_high, per_col, 0)

    prepare(0)
    build_all(0, 1, 0, 1)
    for u in range(1, ru):
        for part in range(2):
            rows_copy(u, 0, part).wait_recv()
        prepare(u)
    build_all(1, ru, 0, 1)
    for u in range(1, cu):
        for part in range(2):
            cols_copy(u, 0, part).wait_recv()
    build_all(0, ru, 1, cu)
    for v in range(1, cv):
        for part in range(2):
            cols_copy(0, v, part).wait_recv()
            for u in range(1, cu):
                cols_copy(u, v, part).start()
    pass_vectors(0)
    for v in range(1, rv):
        for part in range(2):
            rows_copy(0, v, part).wait_recv()
            for u in range(1, ru):
                rows_copy(u, v, part).start()
    build_all(0, ru, cu, cu + 1)
    for v in range(1, rv):
        for u in range(ru):
            if u:
                for part in range(2):
                    rows_copy(u, v, part).wait_recv()
            prepare(v * ru + u)
    build_all(ru, row_count, 0, cu + 1)
    for v in range(1, cv):
        for u in range(1, cu):
            for part in range(2):
                cols_copy(u, v, part).wait_recv()
    build_all(0, row_count, cu + 1, col_count)

    for it in range(ITERS):
        if it:
            pass_vectors(it)
        for u in range(1, cu):
            for v in range(cv):
                vec_copy(it, u, v).wait_recv()
        for i in range(col_count):
            neg_ref[i, :, :width] = -vec_ref[it, i, :, width:]
            neg_ref[i, :, width:] = vec_ref[it, i, :, :width]

        def apply(j):
            def term(i, total):
                total += jnp.dot(tile_ref[j, i, 0], vec_ref[it, i], preferred_element_type=jnp.float32)
                return total + jnp.dot(tile_ref[j, i, 1], neg_ref[i], preferred_element_type=jnp.float32)

            return lax.fori_loop(0, col_count, term, jnp.zeros((own, 2 * width), jnp.float32))

        def send_part(n, carry):
            slot = row_count - n
            rs_send[it, slot - 1] = apply(slot).astype(jnp.bfloat16)
            rs_copy(it, slot).start()
            return carry

        lax.fori_loop(1, row_count, send_part, 0)
        image = apply(0)
        for slot in range(1, row_count):
            rs_copy(it, slot).wait_recv()
            image += rs_recv[it, slot - 1].astype(jnp.float32)

        flat = jnp.concatenate([image[:, :width], image[:, width:]], axis=0)
        gram_send[it] = lax.dot_general(flat, flat, (((0,), (0,)), ((), ())), precision=HIGHEST, preferred_element_type=jnp.float32)
        for step in range(1, nfr):
            gfr_copy(it, step).start()
        gram_fr[it, me_r] = gram_send[it]
        for step in range(1, nfr):
            gfr_copy(it, step).wait_recv()
        gram_mid[it] = jnp.sum(gram_fr[it], axis=0)
        for step in range(1, nfc):
            gfc_copy(it, step).start()
        gram_fc[it, me_c] = gram_mid[it]
        for step in range(1, nfc):
            gfc_copy(it, step).wait_recv()
        gram = jnp.sum(gram_fc[it], axis=0)

        row_id = lax.broadcasted_iota(jnp.int32, (width, width), 0)
        lane_id = lax.broadcasted_iota(jnp.int32, (width, width), 1)
        elim_ref[:, :width] = gram
        elim_ref[:, width:] = jnp.where(row_id == lane_id, 1.0, 0.0)
        size = min(PANEL, width)
        panel_row = lax.broadcasted_iota(jnp.int32, (size, 1), 0)
        for base in range(0, width, size):
            panel = elim_ref[base : base + size, :]
            for n in range(size):
                column = panel[:, base + n : base + n + 1]
                inv = 1.0 / jnp.sqrt(column[n : n + 1, :])
                unit = panel[n : n + 1, :] * inv
                factor = jnp.where(panel_row > n, column * inv, 0.0)
                panel = jnp.where(panel_row == n, unit, panel - factor * unit)
            elim_ref[base : base + size, :] = panel
            rest = base + size
            if rest < width:
                update = lax.dot_general(
                    panel[:, :width], panel, (((0,), (0,)), ((), ())), precision=HIGHEST, preferred_element_type=jnp.float32
                )
                elim_ref[rest:, :] = elim_ref[rest:, :] - update[rest:, :]
        inverse = elim_ref[:, width:]
        vectors = lax.dot_general(flat, inverse, (((1,), (1,)), ((), ())), precision=HIGHEST, preferred_element_type=jnp.float32)
        if it + 1 < ITERS:
            vsend_ref[it + 1, :, :width] = vectors[:own].astype(jnp.bfloat16)
            vsend_ref[it + 1, :, width:] = vectors[own:].astype(jnp.bfloat16)
            send_vectors(it + 1)
        else:
            out_ref[0] = vectors[:own] * scale
            out_ref[1] = vectors[own:] * scale

    for slot in range(1, row_count):
        for part in range(2):
            rows_copy(slot % ru, slot // ru, part).wait_send()
    for slot in range(1, col_count):
        for part in range(2):
            cols_copy(slot % cu, slot // cu, part).wait_send()
    for it in range(ITERS):
        for slot in range(1, col_count):
            vec_copy(it, slot % cu, slot // cu).wait_send()
        for slot in range(1, row_count):
            rs_copy(it, slot).wait_send()
        for step in range(1, nfr):
            gfr_copy(it, step).wait_send()
        for step in range(1, nfc):
            gfc_copy(it, step).wait_send()


def body(nfr, nfc, beam_transfer, noise_var, spectra, freq_covariance, start_vectors):
    _, own_freqs, own_modes, depth = beam_transfer.shape
    own = own_freqs * own_modes
    width = start_vectors.shape[-1]
    order = own_freqs * nfr * own_modes * nfc
    whitened = (beam_transfer.astype(jnp.float32) * lax.rsqrt(noise_var)[None, :, :, None]).astype(jnp.bfloat16)
    position = lax.axis_index("fr")
    row_cov = lax.dynamic_slice_in_dim(freq_covariance, position // PAIR * PAIR * own_freqs, PAIR * own_freqs, 1)
    row_cov = row_cov.reshape(2, PAIR, own_freqs, nfr // PAIR, PAIR, own_freqs)
    row_cov = lax.dynamic_index_in_dim(row_cov, position % PAIR, 4, keepdims=False)
    weight = jnp.transpose(jnp.repeat(row_cov, own_modes, axis=4), (1, 3, 0, 2, 4))
    row_count, col_count = PAIR * (nfc // 2), nfr // PAIR * 2
    bf16, f32 = jnp.bfloat16, jnp.float32
    dma = pltpu.SemaphoreType.DMA
    scratch = [
        pltpu.VMEM((row_count, 2, own, depth), bf16),
        pltpu.VMEM((col_count, 2, own, depth), bf16),
        pltpu.VMEM((row_count, 4, own, 2 * depth), bf16),
        pltpu.VMEM((row_count, col_count, 2, own, own), bf16),
        pltpu.VMEM((ITERS, col_count, own, 2 * width), bf16),
        pltpu.VMEM((col_count, own, 2 * width), bf16),
        pltpu.VMEM((ITERS, own, 2 * width), bf16),
        pltpu.VMEM((ITERS, row_count - 1, own, 2 * width), bf16),
        pltpu.VMEM((ITERS, row_count - 1, own, 2 * width), bf16),
        pltpu.VMEM((ITERS, width, width), f32),
        pltpu.VMEM((ITERS, nfr, width, width), f32),
        pltpu.VMEM((ITERS, width, width), f32),
        pltpu.VMEM((ITERS, nfc, width, width), f32),
        pltpu.VMEM((width, 2 * width), f32),
        dma((row_count - 1, 2)), dma((row_count - 1, 2)), dma((col_count - 1, 2)), dma((col_count - 1, 2)),
        dma((ITERS, col_count - 1)), dma((ITERS, col_count - 1)), dma((ITERS, row_count - 1)), dma((ITERS, row_count - 1)),
        dma((ITERS, nfr - 1)), dma((ITERS, nfr - 1)), dma((ITERS, nfc - 1)), dma((ITERS, nfc - 1)),
    ]
    vmem = pl.BlockSpec(memory_space=pltpu.VMEM)
    basis = pl.pallas_call(
        functools.partial(kernel, nfr, nfc, own_modes, math.sqrt(2.0 * order)),
        out_shape=jax.ShapeDtypeStruct((2, own, width), f32),
        in_specs=[vmem] * 4,
        out_specs=vmem,
        scratch_shapes=scratch,
        compiler_params=pltpu.CompilerParams(
            collective_id=0, has_side_effects=True, vmem_limit_bytes=60 * 1024 * 1024
        ),
    )(whitened.reshape(2, own, depth), weight, spectra, start_vectors.reshape(2, own, width))
    return basis.reshape(start_vectors.shape)


def solution(mesh):
    spec = P(None, ("ma", "fr"), "fc", None)
    in_specs = (spec, P(("ma", "fr"), "fc"), P(), P(), spec)
    run = functools.partial(body, mesh.shape["fr"], mesh.shape["fc"])
    return jax.shard_map(run, mesh=mesh, in_specs=in_specs, out_specs=spec, check_vma=False)
```

```python
import functools
import math

import jax
import jax.numpy as jnp
from jax import lax
from jax.experimental import pallas as pl
from jax.experimental.pallas import tpu as pltpu
from jax.sharding import PartitionSpec as P

ITERS = 2
MESH = pl.DeviceIdType.MESH
HIGHEST = lax.Precision.HIGHEST


PAIR = 2
PANEL = 32


def partner(me, step, count):
    total = 0
    bit = 1
    while bit < count:
        total = total + ((me // bit + step // bit) % 2) * bit
        bit *= 2
    return total


def kernel(
    nfr, nfc, own_modes, scale,
    w_ref, weight_ref, spec_ref, start_ref, out_ref,
    rows_ref, cols_ref, oper_ref, tile_ref, vec_ref, neg_ref, vsend_ref,
    rs_send, rs_recv, gram_send, gram_fr, gram_mid, gram_fc, elim_ref,
    rows_ss, rows_rs, cols_ss, cols_rs, vec_ss, vec_rs, rs_ss, rs_rs,
    gfr_ss, gfr_rs, gfc_ss, gfc_rs,
):
    me_r = lax.axis_index("fr")
    me_c = lax.axis_index("fc")
    own, depth = w_ref.shape[1], w_ref.shape[2]
    width = start_ref.shape[-1]
    block_rows = min(256, own)
    block_freqs = block_rows // own_modes
    ru, rv = PAIR, nfc // 2
    cu, cv = nfr // PAIR, 2
    row_count, col_count = ru * rv, cu * cv
    low_r, high_r = me_r % PAIR, me_r // PAIR
    low_c, high_c = me_c % rv, me_c // rv

    def row_peer(u, v):
        return {"fr": high_r * PAIR + partner(low_r, u, ru), "fc": high_c * rv + partner(low_c, v, rv)}

    def col_peer(u, v):
        return {"fr": partner(high_r, u, cu) * PAIR + low_r, "fc": partner(high_c, v, cv) * rv + low_c}

    def copy(src, dst, ss, rs, peer):
        return pltpu.make_async_remote_copy(
            src_ref=src, dst_ref=dst, send_sem=ss, recv_sem=rs, device_id=peer, device_id_type=MESH
        )

    barrier = pltpu.get_barrier_semaphore()
    greet = [{"fr": partner(me_r, step, nfr)} for step in range(1, nfr)]
    greet += [{"fc": partner(me_c, step, nfc)} for step in range(1, nfc)]
    greet += [row_peer(u, v) for u in range(1, ru) for v in range(1, rv)]
    for peer in greet:
        pl.semaphore_signal(barrier, inc=1, device_id=peer, device_id_type=MESH)
    pl.semaphore_wait(barrier, len(greet))

    def rows_copy(u, v, part):
        src = w_ref.at[part] if u == 0 or v == 0 else rows_ref.at[v * ru, part]
        slot = v * ru + u
        peer = row_peer(0, v) if u == 0 else row_peer(u, 0)
        return copy(src, rows_ref.at[slot, part], rows_ss.at[slot - 1, part], rows_rs.at[slot - 1, part], peer)

    def cols_copy(u, v, part):
        src = w_ref.at[part] if u == 0 or v == 0 else cols_ref.at[v * cu, part]
        slot = v * cu + u
        peer = col_peer(0, v) if u == 0 else col_peer(u, 0)
        return copy(src, cols_ref.at[slot, part], cols_ss.at[slot - 1, part], cols_rs.at[slot - 1, part], peer)

    def vec_copy(it, u, v, part):
        half = pl.ds(part * (own // 2), own // 2)
        src = vsend_ref.at[it, half] if u == 0 or v == 0 else vec_ref.at[it, v * cu, half]
        slot = v * cu + u
        peer = col_peer(0, v) if u == 0 else col_peer(u, 0)
        return copy(src, vec_ref.at[it, slot, half], vec_ss.at[it, slot - 1, part], vec_rs.at[it, slot - 1, part], peer)

    def rs_copy(it, slot):
        return copy(
            rs_send.at[it, slot - 1], rs_recv.at[it, slot - 1], rs_ss.at[it, slot - 1], rs_rs.at[it, slot - 1],
            row_peer(slot % ru, slot // ru),
        )

    def gfr_copy(it, step):
        peer = partner(me_r, step, nfr)
        return copy(gram_send.at[it], gram_fr.at[it, me_r], gfr_ss.at[it, step - 1], gfr_rs.at[it, step - 1], {"fr": peer})

    def gfc_copy(it, step):
        peer = partner(me_c, step, nfc)
        return copy(gram_mid.at[it], gram_fc.at[it, me_c], gfc_ss.at[it, step - 1], gfc_rs.at[it, step - 1], {"fc": peer})

    def send_vectors(it):
        for v in range(1, cv):
            for part in range(2):
                vec_copy(it, 0, v, part).start()
        for u in range(1, cu):
            for part in range(2):
                vec_copy(it, u, 0, part).start()
        vec_ref[it, 0] = vsend_ref[it]

    def pass_vectors(it):
        for v in range(1, cv):
            for part in range(2):
                vec_copy(it, 0, v, part).wait_recv()
                for u in range(1, cu):
                    vec_copy(it, u, v, part).start()

    for v in range(1, rv):
        for part in range(2):
            rows_copy(0, v, part).start()
    for v in range(1, cv):
        for part in range(2):
            cols_copy(0, v, part).start()
    for u in range(1, cu):
        for part in range(2):
            cols_copy(u, 0, part).start()
    for u in range(1, ru):
        for part in range(2):
            rows_copy(u, 0, part).start()
    vsend_ref[0, :, :width] = start_ref[0].astype(jnp.bfloat16)
    vsend_ref[0, :, width:] = start_ref[1].astype(jnp.bfloat16)
    send_vectors(0)
    rows_ref[0] = w_ref[...]
    cols_ref[0] = w_ref[...]

    def prepare(j):
        for k in range(2):
            spec = spec_ref[k : k + 1, :]
            real = (rows_ref[j, 0].astype(jnp.float32) * spec).astype(jnp.bfloat16)
            imag = (rows_ref[j, 1].astype(jnp.float32) * spec).astype(jnp.bfloat16)
            oper_ref[j, 2 * k, :, :depth] = real
            oper_ref[j, 2 * k, :, depth:] = imag
            oper_ref[j, 2 * k + 1, :, :depth] = imag
            oper_ref[j, 2 * k + 1, :, depth:] = -real

    def build(j, i):
        row_weight = partner(low_r, j % ru, ru)
        col_weight = partner(high_r, i % cu, cu)

        def part(b, carry):
            rows = pl.ds(pl.multiple_of(b * block_rows, block_rows), block_rows)
            left = oper_ref[j, :, rows, :].reshape(4 * block_rows, 2 * depth)
            prod = lax.dot_general(left[:, :depth], cols_ref[i, 0], (((1,), (1,)), ((), ())), preferred_element_type=jnp.float32)
            prod += lax.dot_general(left[:, depth:], cols_ref[i, 1], (((1,), (1,)), ((), ())), preferred_element_type=jnp.float32)
            prod = prod.reshape(4, block_rows, own)
            freqs = pl.ds(pl.multiple_of(b * block_freqs, block_freqs), block_freqs)
            first, second = (
                jnp.broadcast_to(
                    weight_ref[row_weight, col_weight, k, freqs, :][:, None, :], (block_freqs, own_modes, own)
                ).reshape(block_rows, own)
                for k in range(2)
            )
            for c in range(2):
                tile_ref[j, i, c, rows, :] = (first * prod[c] + second * prod[2 + c]).astype(jnp.bfloat16)
            return carry

        lax.fori_loop(0, own // block_rows, part, 0)

    def build_all(row_low, row_high, col_low, col_high):
        def per_col(i, carry):
            def per_row(j, inner):
                build(j, i)
                return inner

            return lax.fori_loop(row_low, row_high, per_row, carry)

        lax.fori_loop(col_low, col_high, per_col, 0)

    prepare(0)
    build_all(0, 1, 0, 1)
    for u in range(1, ru):
        for part in range(2):
            rows_copy(u, 0, part).wait_recv()
        prepare(u)
    build_all(1, ru, 0, 1)
    for u in range(1, cu):
        for part in range(2):
            cols_copy(u, 0, part).wait_recv()
    build_all(0, ru, 1, cu)
    for v in range(1, rv):
        for part in range(2):
            rows_copy(0, v, part).wait_recv()
            for u in range(1, ru):
                rows_copy(u, v, part).start()
        prepare(v * ru)
    for v in range(1, rv):
        build_all(v * ru, v * ru + 1, 0, cu)
    for v in range(1, cv):
        for part in range(2):
            cols_copy(0, v, part).wait_recv()
            for u in range(1, cu):
                cols_copy(u, v, part).start()
    for v in range(1, rv):
        for u in range(1, ru):
            for part in range(2):
                rows_copy(u, v, part).wait_recv()
            prepare(v * ru + u)
    for v in range(1, rv):
        build_all(v * ru + 1, v * ru + ru, 0, cu)
    pass_vectors(0)
    build_all(0, row_count, cu, cu + 1)
    for v in range(1, cv):
        for u in range(1, cu):
            for part in range(2):
                cols_copy(u, v, part).wait_recv()
    build_all(0, row_count, cu + 1, col_count)

    for it in range(ITERS):
        if it:
            pass_vectors(it)
        for u in range(1, cu):
            for v in range(cv):
                for part in range(2):
                    vec_copy(it, u, v, part).wait_recv()
        for i in range(col_count):
            neg_ref[i, :, :width] = -vec_ref[it, i, :, width:]
            neg_ref[i, :, width:] = vec_ref[it, i, :, :width]

        def apply(j):
            def term(i, total):
                total += jnp.dot(tile_ref[j, i, 0], vec_ref[it, i], preferred_element_type=jnp.float32)
                return total + jnp.dot(tile_ref[j, i, 1], neg_ref[i], preferred_element_type=jnp.float32)

            return lax.fori_loop(0, col_count, term, jnp.zeros((own, 2 * width), jnp.float32))

        def send_part(n, carry):
            slot = row_count - n
            rs_send[it, slot - 1] = apply(slot).astype(jnp.bfloat16)
            rs_copy(it, slot).start()
            return carry

        lax.fori_loop(1, row_count, send_part, 0)
        image = apply(0)
        for slot in range(1, row_count):
            rs_copy(it, slot).wait_recv()
            image += rs_recv[it, slot - 1].astype(jnp.float32)

        flat = jnp.concatenate([image[:, :width], image[:, width:]], axis=0)
        gram_send[it] = lax.dot_general(flat, flat, (((0,), (0,)), ((), ())), precision=HIGHEST, preferred_element_type=jnp.float32)
        for step in range(1, nfr):
            gfr_copy(it, step).start()
        gram_fr[it, me_r] = gram_send[it]
        for step in range(1, nfr):
            gfr_copy(it, step).wait_recv()
        gram_mid[it] = jnp.sum(gram_fr[it], axis=0)
        for step in range(1, nfc):
            gfc_copy(it, step).start()
        gram_fc[it, me_c] = gram_mid[it]
        for step in range(1, nfc):
            gfc_copy(it, step).wait_recv()
        gram = jnp.sum(gram_fc[it], axis=0)

        row_id = lax.broadcasted_iota(jnp.int32, (width, width), 0)
        lane_id = lax.broadcasted_iota(jnp.int32, (width, width), 1)
        elim_ref[:, :width] = gram
        elim_ref[:, width:] = jnp.where(row_id == lane_id, 1.0, 0.0)
        size = min(PANEL, width)
        panel_row = lax.broadcasted_iota(jnp.int32, (size, 1), 0)
        for base in range(0, width, size):
            panel = elim_ref[base : base + size, :]
            for n in range(size):
                column = panel[:, base + n : base + n + 1]
                inv = lax.rsqrt(column[n : n + 1, :])
                unit = panel[n : n + 1, :] * inv
                factor = jnp.where(panel_row > n, column * inv, 0.0)
                panel = jnp.where(panel_row == n, unit, panel - factor * unit)
            elim_ref[base : base + size, :] = panel
            rest = base + size
            if rest < width:
                update = lax.dot_general(
                    panel[:, :width], panel, (((0,), (0,)), ((), ())), precision=HIGHEST, preferred_element_type=jnp.float32
                )
                elim_ref[rest:, :] = elim_ref[rest:, :] - update[rest:, :]
        inverse = elim_ref[:, width:]
        vectors = lax.dot_general(flat, inverse, (((1,), (1,)), ((), ())), precision=HIGHEST, preferred_element_type=jnp.float32)
        if it + 1 < ITERS:
            vsend_ref[it + 1, :, :width] = vectors[:own].astype(jnp.bfloat16)
            vsend_ref[it + 1, :, width:] = vectors[own:].astype(jnp.bfloat16)
            send_vectors(it + 1)
        else:
            out_ref[0] = vectors[:own] * scale
            out_ref[1] = vectors[own:] * scale

    for slot in range(1, row_count):
        for part in range(2):
            rows_copy(slot % ru, slot // ru, part).wait_send()
    for slot in range(1, col_count):
        for part in range(2):
            cols_copy(slot % cu, slot // cu, part).wait_send()
    for it in range(ITERS):
        for slot in range(1, col_count):
            for part in range(2):
                vec_copy(it, slot % cu, slot // cu, part).wait_send()
        for slot in range(1, row_count):
            rs_copy(it, slot).wait_send()
        for step in range(1, nfr):
            gfr_copy(it, step).wait_send()
        for step in range(1, nfc):
            gfc_copy(it, step).wait_send()


def body(nfr, nfc, beam_transfer, noise_var, spectra, freq_covariance, start_vectors):
    _, own_freqs, own_modes, depth = beam_transfer.shape
    own = own_freqs * own_modes
    width = start_vectors.shape[-1]
    order = own_freqs * nfr * own_modes * nfc
    whitened = (beam_transfer.astype(jnp.float32) * lax.rsqrt(noise_var)[None, :, :, None]).astype(jnp.bfloat16)
    position = lax.axis_index("fr")
    row_cov = lax.dynamic_slice_in_dim(freq_covariance, position // PAIR * PAIR * own_freqs, PAIR * own_freqs, 1)
    row_cov = row_cov.reshape(2, PAIR, own_freqs, nfr // PAIR, PAIR, own_freqs)
    row_cov = lax.dynamic_index_in_dim(row_cov, position % PAIR, 4, keepdims=False)
    weight = jnp.transpose(jnp.repeat(row_cov, own_modes, axis=4), (1, 3, 0, 2, 4))
    row_count, col_count = PAIR * (nfc // 2), nfr // PAIR * 2
    bf16, f32 = jnp.bfloat16, jnp.float32
    dma = pltpu.SemaphoreType.DMA
    scratch = [
        pltpu.VMEM((row_count, 2, own, depth), bf16),
        pltpu.VMEM((col_count, 2, own, depth), bf16),
        pltpu.VMEM((row_count, 4, own, 2 * depth), bf16),
        pltpu.VMEM((row_count, col_count, 2, own, own), bf16),
        pltpu.VMEM((ITERS, col_count, own, 2 * width), bf16),
        pltpu.VMEM((col_count, own, 2 * width), bf16),
        pltpu.VMEM((ITERS, own, 2 * width), bf16),
        pltpu.VMEM((ITERS, row_count - 1, own, 2 * width), bf16),
        pltpu.VMEM((ITERS, row_count - 1, own, 2 * width), bf16),
        pltpu.VMEM((ITERS, width, width), f32),
        pltpu.VMEM((ITERS, nfr, width, width), f32),
        pltpu.VMEM((ITERS, width, width), f32),
        pltpu.VMEM((ITERS, nfc, width, width), f32),
        pltpu.VMEM((width, 2 * width), f32),
        dma((row_count - 1, 2)), dma((row_count - 1, 2)), dma((col_count - 1, 2)), dma((col_count - 1, 2)),
        dma((ITERS, col_count - 1, 2)), dma((ITERS, col_count - 1, 2)), dma((ITERS, row_count - 1)), dma((ITERS, row_count - 1)),
        dma((ITERS, nfr - 1)), dma((ITERS, nfr - 1)), dma((ITERS, nfc - 1)), dma((ITERS, nfc - 1)),
    ]
    vmem = pl.BlockSpec(memory_space=pltpu.VMEM)
    basis = pl.pallas_call(
        functools.partial(kernel, nfr, nfc, own_modes, math.sqrt(2.0 * order)),
        out_shape=jax.ShapeDtypeStruct((2, own, width), f32),
        in_specs=[vmem] * 4,
        out_specs=vmem,
        scratch_shapes=scratch,
        compiler_params=pltpu.CompilerParams(
            collective_id=0, has_side_effects=True, vmem_limit_bytes=60 * 1024 * 1024
        ),
    )(whitened.reshape(2, own, depth), weight, spectra, start_vectors.reshape(2, own, width))
    return basis.reshape(start_vectors.shape)


def solution(mesh):
    spec = P(None, ("ma", "fr"), "fc", None)
    in_specs = (spec, P(("ma", "fr"), "fc"), P(), P(), spec)
    run = functools.partial(body, mesh.shape["fr"], mesh.shape["fc"])
    return jax.shard_map(run, mesh=mesh, in_specs=in_specs, out_specs=spec, check_vma=False)
```
